32 devices in a mesh: dp: 8 (over z, x), ctx: 4 (over y, core).
Axes of the slice: x: 2, y: 2, z: 4, core: 2. Of those that a mesh axis runs over, the one named last changes fastest.
Arguments:
- queries: bfloat16 [8, 2048, 1280], P('dp', 'ctx'), may hold values from -14 to 14
- own_keys: bfloat16 [8, 2048, 1280], P('dp', 'ctx'), may hold values from -6 to 6
- own_values: bfloat16 [8, 2048, 1280], P('dp', 'ctx'), may hold values from -12 to 12
- variant_blocks: int32 [8, 4, 6], P('dp', 'ctx'), may hold values from 1 to 2, 8 in all within a row
- db_keys: bfloat16 [8, 256, 1280], P('dp', 'ctx'), may hold values from -6 to 6
- db_values: bfloat16 [8, 256, 1280], P('dp', 'ctx'), may hold values from -12 to 12
- ret_shard: int32 [8, 64], P(None, 'ctx'), may hold values from 0 to 7, as said below
- ret_block: int32 [8, 64], P(None, 'ctx'), may hold values from 0 to 15
Outputs:
- attended: bfloat16 [8, 2048, 1280], P('dp', 'ctx')
The draws below stay inside these ranges and needn't reach their ends.
Inputs may be any that keep to these rules, and one draw needn't show every extreme that they name: `ret_shard`: within each aligned block of 16 entries of a row (the retrieval blocks of one context device), no shard is named more than 4 times, and some shard is named exactly 4 times.
All inputs are finite; a program needn't handle non-finite values.
Results may differ from the reference program's by a relative error of at most 0.0035.
Values may be sent and summed in bfloat16 or wider, within the bound.
No kernel may reach another device: no remote copies, remote signals or barrier semaphores. Data moves between devices by JAX's collectives and lax.ppermute only.
A program may use at most 192 MiB of HBM per device.

```python
import math
import jax
import jax.numpy as jnp
import numpy as np
from jax import lax

HEADS = 10
HEAD_DIM = 128
BLK = 64
ROW_BLK = 4
VAR_MOST = 2
TOK_DEV = 64
Q_DEV = 512
SLOTS = 16
MOST = 4
VARS = 6
CONTEXT = 256
QUERIES = 2048
N_DP = 8
N_CTX = 4


def draw_queries(key, part):
    shape = (N_DP, N_CTX * Q_DEV, HEADS * HEAD_DIM)
    drawn = jnp.clip(2.0 * jax.random.normal(jax.random.fold_in(key, 11), shape, jnp.float32), -12.0, 12.0)
    return drawn.astype(jnp.bfloat16)


def draw_db_keys(key, part):
    shape = (N_DP, N_CTX * TOK_DEV, HEADS * HEAD_DIM)
    drawn = jnp.clip(jax.random.normal(jax.random.fold_in(key, 21), shape, jnp.float32), -6.0, 6.0)
    return drawn.astype(jnp.bfloat16)


def draw_ret_shard(key, part):

    def per_device(device_key):
        first_key, second_key, third_key = jax.random.split(device_key, 3)
        owner = jax.random.permutation(first_key, N_DP).astype(jnp.int32)
        others = (MOST + jax.random.permutation(second_key, N_DP * MOST - MOST)).astype(jnp.int32)
        chosen = jnp.concatenate([jnp.arange(MOST, dtype=jnp.int32), others[:SLOTS - MOST]])
        shards = owner[chosen // MOST]
        return shards[jax.random.permutation(third_key, SLOTS)].astype(jnp.int32)
    device_keys = jax.random.split(jax.random.fold_in(key, 31), N_DP * N_CTX)
    table = jax.vmap(per_device)(device_keys)
    return table.reshape(N_DP, N_CTX * SLOTS).astype(jnp.int32)


def with_ends(drawn, own_key, smallest, largest):
    place = [jax.random.randint(jax.random.fold_in(own_key, axis), (), 0, length) for axis, length in enumerate(drawn.shape)]
    main_axis = drawn.shape.index(max(drawn.shape))
    beside = place[:main_axis] + [(place[main_axis] + 1) % drawn.shape[main_axis]] + place[main_axis + 1:]
    return drawn.at[tuple(place)].set(smallest).at[tuple(beside)].set(largest)


def block_scale(rng, extent, pieces, low, high):
    factor_of = 1.0
    for dim, parts in pieces:
        steps = jax.random.uniform(jax.random.fold_in(jax.random.fold_in(rng, 6), dim), (parts,), jnp.float32, low / len(pieces), high / len(pieces))
        factor_of = factor_of * jnp.repeat(jnp.exp(steps), extent[dim] // parts).reshape((-1,) + (1,) * (len(extent) - 1 - dim))
    return factor_of


def length_profile(amount, total, reach, skew):
    portions = [(1 << 20) // math.isqrt(standing ** skew) + 1 for standing in range(2, amount + 1)]
    surplus, counts = total - reach - (amount - 1), [1] * (amount - 1)
    while surplus > 0:
        candidates = [i for i in range(amount - 1) if counts[i] < reach]
        mass, left = sum([portions[i] for i in candidates]), surplus
        for i in candidates:
            extra = min(reach - counts[i], max(1, left * portions[i] // mass), surplus)
            counts[i] = counts[i] + extra
            surplus = surplus - extra
    return np.array([reach] + counts)


def uneven(stream_key, amount, total, most, skew):
    if amount == 2:
        one = jax.random.randint(stream_key, (), max(1, total - most), min(most, total - 1) + 1)
        return jnp.stack([one, total - one])
    tallies = jnp.asarray(length_profile(amount, total, most, skew), jnp.int32)
    pairs = (amount - 1) // 2
    giver, receiver = tallies[1:1 + 2 * pairs:2], tallies[2:2 + 2 * pairs:2]
    slack = jnp.minimum(giver - 1, most - receiver)
    moved = jax.random.randint(jax.random.fold_in(stream_key, 1), (pairs,), 0, 1 << 20) % (slack + 1)
    tallies = tallies.at[1:1 + 2 * pairs:2].set(giver - moved).at[2:2 + 2 * pairs:2].set(receiver + moved)
    return tallies[jax.random.permutation(jax.random.fold_in(stream_key, 2), amount)]


def scatter_about(key, shape, spread, reach, cuts=(), kind=jnp.bfloat16):
    array = jax.random.normal(key, shape, jnp.float32) * spread
    if len(cuts) > 0:
        array = block_scale(key, shape, cuts, -0.22, 0.18) * array
    return jnp.clip(array, min=-reach, max=reach).astype(kind)


def setup_inputs(seed: int = 0) -> dict:
    splits = jax.random.split(jax.random.key(seed), 9)
    queries = draw_queries(jax.random.fold_in(splits[8], 71), 0)
    own_keys = scatter_about(splits[1], (N_DP, QUERIES, HEADS * HEAD_DIM), 1.0, 6.0, ((0, 8), (1, 4)))
    own_values = scatter_about(splits[2], (N_DP, QUERIES, HEADS * HEAD_DIM), 2.0, 12.0, ((0, 8), (1, 4)))
    variant_blocks = jax.vmap(lambda own: uneven(own, VARS, Q_DEV // BLK, VAR_MOST, 0))(jax.random.split(splits[3], N_DP * N_CTX)).reshape((N_DP, N_CTX, VARS)).astype(jnp.int32)
    db_keys = draw_db_keys(jax.random.fold_in(splits[8], 71), 0)
    db_values = scatter_about(splits[5], (N_DP, CONTEXT, HEADS * HEAD_DIM), 2.0, 12.0, ((0, 8), (1, 4)))
    ret_shard = draw_ret_shard(jax.random.fold_in(splits[8], 71), 0)
    ret_block = with_ends(jax.random.randint(splits[7], (N_DP, N_CTX * SLOTS), 0, SLOTS), jax.random.fold_in(splits[7], 1), 0, SLOTS - 1).astype(jnp.int32)
    return dict(queries=queries, own_keys=own_keys, own_values=own_values, variant_blocks=variant_blocks, db_keys=db_keys, db_values=db_values, ret_shard=ret_shard, ret_block=ret_block)


masked_score = -1e+30

def reference(queries, own_keys, own_values, variant_blocks, db_keys, db_values, ret_shard, ret_block):
    features = queries.shape[2]
    head_count = features // HEAD_DIM
    slot_count = TOK_DEV // ROW_BLK
    column = (jnp.arange(N_CTX * slot_count, dtype=jnp.int32) // slot_count).astype(jnp.int32)
    block_start = ret_shard * (N_CTX * TOK_DEV) + column[None, :] * TOK_DEV + ret_block * ROW_BLK
    context_rows = (block_start[:, :, None] + jnp.arange(ROW_BLK, dtype=jnp.int32)[None, None, :]).reshape(N_DP, N_CTX * TOK_DEV).astype(jnp.int32)
    flat_keys = db_keys.reshape(N_DP * N_CTX * TOK_DEV, features)
    flat_values = db_values.reshape(N_DP * N_CTX * TOK_DEV, features)
    positions = jnp.arange(Q_DEV, dtype=jnp.int32)
    causal = positions[None, :] <= positions[:, None]

    def per_device(device_index):
        group_index = (device_index // N_CTX).astype(jnp.int32)
        column_index = (device_index % N_CTX).astype(jnp.int32)
        rows_here = lax.dynamic_index_in_dim(context_rows, group_index, 0, keepdims=False)
        ctx_keys = jnp.take(flat_keys, rows_here, axis=0).astype(jnp.float32)
        ctx_values = jnp.take(flat_values, rows_here, axis=0).astype(jnp.float32)
        start_row = (column_index * Q_DEV).astype(jnp.int32)

        def own_rows(source):
            whole = lax.dynamic_index_in_dim(source, group_index, 0, keepdims=False)
            return lax.dynamic_slice_in_dim(whole, start_row, Q_DEV, 0).astype(jnp.float32)
        query_rows = own_rows(queries)
        key_rows = own_rows(own_keys)
        value_rows = own_rows(own_values)
        lengths = lax.dynamic_index_in_dim(lax.dynamic_index_in_dim(variant_blocks, group_index, 0, keepdims=False), column_index, 0, keepdims=False)
        variant_ends = jnp.cumsum(lengths) * BLK
        segment = lax.optimization_barrier(jnp.sum((variant_ends[None, :] <= positions[:, None]).astype(jnp.int32), axis=1))
        allowed_own = (segment[None, :] == segment[:, None]) & causal
        all_keys = jnp.concatenate([ctx_keys, key_rows], axis=0).reshape(-1, head_count, HEAD_DIM)
        all_values = jnp.concatenate([ctx_values, value_rows], axis=0).reshape(-1, head_count, HEAD_DIM)
        allowed = jnp.concatenate([jnp.ones((Q_DEV, N_CTX * TOK_DEV), dtype=bool), allowed_own], axis=1)
        scores = jnp.einsum('qhd,khd->hqk', query_rows.reshape(Q_DEV, head_count, HEAD_DIM), all_keys, precision=lax.Precision.HIGHEST) * (1.0 / math.sqrt(HEAD_DIM))
        scores = jnp.where(allowed[None], scores, masked_score)
        row_max = lax.optimization_barrier(jnp.max(scores, axis=2, keepdims=True))
        weights = jnp.where(allowed[None], jnp.exp(scores - row_max), 0.0)
        row_total = lax.optimization_barrier(jnp.sum(weights, axis=2))
        rounded = lax.optimization_barrier(weights.astype(jnp.bfloat16)).astype(jnp.float32)
        weighted = jnp.einsum('hqk,khd->hqd', rounded, all_values, precision=lax.Precision.HIGHEST)
        result_rows = weighted / row_total[:, :, None]
        return jnp.transpose(result_rows, (1, 0, 2)).reshape(Q_DEV, features).astype(jnp.bfloat16)
    result = lax.map(per_device, jnp.arange(N_DP * N_CTX, dtype=jnp.int32))
    return result.reshape(N_DP, N_CTX * Q_DEV, features)
```

```python
import math

import jax
import jax.numpy as jnp
from jax import lax
from jax.experimental import pallas as pl
from jax.experimental.pallas import tpu as pltpu
from jax.sharding import PartitionSpec as P

HEAD_DIM = 128
BLK = 64
ROW_BLK = 4
VAR_MOST = 2


SMEM = pl.BlockSpec(memory_space=pltpu.SMEM)
VMEM = pl.BlockSpec(memory_space=pltpu.VMEM)
masked_score = -1e30


def iota(shape, dim):
    return lax.broadcasted_iota(jnp.int32, shape, dim)


def pick(matrix, rows):
    return jnp.dot(matrix.astype(jnp.bfloat16), rows, preferred_element_type=jnp.float32).astype(
        jnp.bfloat16
    )


def pack_kernel(capacity, me_ref, shard_ref, block_ref, keys_ref, values_ref, *out_refs):
    me = me_ref[0]
    slots = shard_ref.shape[1]
    tokens = keys_ref.shape[0]
    half = capacity * ROW_BLK
    rows = jnp.concatenate([keys_ref[...], values_ref[...]], axis=0)
    row = iota((2 * half, slots), 0)
    slot = iota((2 * half, slots), 1)
    level = (row % half) // ROW_BLK
    before = (iota((slots, slots), 0) < iota((slots, slots), 1)).astype(jnp.float32)
    mine_all = (shard_ref[...] == me).astype(jnp.float32)
    earlier_all = jnp.dot(mine_all, before, preferred_element_type=jnp.float32)
    wanted_all = jnp.where(mine_all > 0, earlier_all.astype(jnp.int32), -1)
    line = iota((2 * half, 1), 0)
    base = (line // half) * tokens + line % ROW_BLK
    column = iota((2 * half, 2 * tokens), 1)
    member = iota(wanted_all.shape, 0)
    for distance, out_ref in enumerate(out_refs):
        group = me ^ distance
        here = member == group
        wanted = jnp.sum(jnp.where(here, wanted_all, 0), axis=0, keepdims=True)
        blocks = jnp.sum(jnp.where(here, block_ref[...], 0), axis=0, keepdims=True)
        source = jnp.sum(jnp.where(wanted == level, blocks, 0), axis=1, keepdims=True)
        out_ref[...] = pick(column == base + source * ROW_BLK, rows)


def compact_kernel(capacity, me_ref, shard_ref, *refs):
    piece_refs, (keys_ref, values_ref) = refs[:-2], refs[-2:]
    me = me_ref[0]
    slots = shard_ref.shape[1]
    half = capacity * ROW_BLK
    tokens = slots * ROW_BLK
    pieces = jnp.concatenate([piece_ref[...] for piece_ref in piece_refs], axis=0)
    here = iota(shard_ref.shape, 0) == me
    shards = jnp.sum(jnp.where(here, shard_ref[...], 0), axis=0, keepdims=True)
    slot = iota((tokens, slots), 0) // ROW_BLK
    lane = iota((tokens, slots), 1)
    named = jnp.sum(jnp.where(lane == slot, shards, 0), axis=1, keepdims=True)
    level = jnp.sum(((shards == named) & (lane < slot)).astype(jnp.int32), axis=1, keepdims=True)
    inside = iota((tokens, 1), 0) % ROW_BLK
    target = (named ^ me) * (2 * half) + level * ROW_BLK + inside
    column = iota((tokens, pieces.shape[0]), 1)
    keys_ref[...] = pick(column == target, pieces)
    values_ref[...] = pick(column == target + half, pieces)


def score_kernel(lengths_ref, q_ref, own_keys_ref, own_values_ref, *refs):
    key_refs, (acc_ref, weights_ref, inverse_ref, mask_ref) = refs[:-4], refs[-4:]
    head = pl.program_id(0)
    count = q_ref.shape[0]
    blocks = count // BLK
    starts = [max(0, block - 1) for block in range(blocks)]

    @pl.when(head == 0)
    def _():
        inverse_ref[...] = jnp.zeros_like(inverse_ref)
        row = iota((BLK, 2 * BLK), 0)
        column = iota((BLK, 2 * BLK), 1)
        mask_ref[0:BLK, :] = jnp.where(column <= row, 0.0, masked_score)
        for block in range(1, blocks):
            end = jnp.int32(0)
            opens = jnp.int32(0)
            for variant in range(lengths_ref.shape[0]):
                end = end + lengths_ref[variant]
                opens = opens + (end == block).astype(jnp.int32)
            first = jnp.where(opens > 0, BLK, 0)
            allowed = (column <= row + BLK) & (column >= first)
            mask_ref[block * BLK : (block + 1) * BLK, :] = jnp.where(allowed, 0.0, masked_score)

    scale = math.log2(math.e) / math.sqrt(HEAD_DIM)
    nt = (((1,), (1,)), ((), ()))
    query = q_ref[...]
    keys = jnp.concatenate([key_ref[...] for key_ref in key_refs], axis=0)
    scores = lax.dot_general(query, keys, nt, preferred_element_type=jnp.float32) * scale
    own = jnp.concatenate(
        [
            lax.dot_general(
                query[block * BLK : (block + 1) * BLK],
                own_keys_ref[starts[block] * BLK : (starts[block] + 2) * BLK, :],
                nt,
                preferred_element_type=jnp.float32,
            )
            for block in range(blocks)
        ],
        axis=0,
    )
    own = own * scale + mask_ref[...]
    largest = jnp.maximum(
        jnp.max(scores, axis=1, keepdims=True), jnp.max(own, axis=1, keepdims=True)
    )
    weights = jnp.exp2(scores - largest)
    own_weights = jnp.exp2(own - largest)
    total = jnp.sum(weights, axis=1, keepdims=True) + jnp.sum(own_weights, axis=1, keepdims=True)
    weights_ref[0] = weights.astype(jnp.bfloat16)
    own_weights = own_weights.astype(jnp.bfloat16)
    acc_ref[...] = jnp.concatenate(
        [
            jnp.dot(
                own_weights[block * BLK : (block + 1) * BLK],
                own_values_ref[starts[block] * BLK : (starts[block] + 2) * BLK, :],
                preferred_element_type=jnp.float32,
            )
            for block in range(blocks)
        ],
        axis=0,
    )
    lane = iota(inverse_ref.shape, 1)
    inverse_ref[...] = jnp.where(lane == head, 1.0 / total, inverse_ref[...])


def value_kernel(acc_ref, weights_ref, inverse_ref, *refs):
    value_refs, out_ref = refs[:-1], refs[-1]
    head = pl.program_id(0)
    values = jnp.concatenate([value_ref[...] for value_ref in value_refs], axis=0)
    lane = iota(inverse_ref.shape, 1)
    inverse = jnp.sum(jnp.where(lane == head, inverse_ref[...], 0.0), axis=1, keepdims=True)
    attended = acc_ref[...] + jnp.dot(
        weights_ref[0], values, preferred_element_type=jnp.float32
    )
    out_ref[...] = (attended * inverse).astype(out_ref.dtype)


def swap(array, axis, distance):
    size = lax.axis_size(axis)
    return lax.ppermute(array, axis, [(i, i ^ distance) for i in range(size)])


def per_device(
    queries, own_keys, own_values, variant_blocks, db_keys, db_values, ret_shard, ret_block
):
    count, features = queries.shape[1:]
    heads = features // HEAD_DIM
    groups = lax.axis_size("dp")
    columns = lax.axis_size("ctx")
    slots = ret_shard.shape[1]
    tokens = slots * ROW_BLK
    capacity = max(2, 2 * slots // groups)
    me = lax.axis_index("dp").astype(jnp.int32).reshape(1)
    bf16 = jnp.bfloat16
    piece = jax.ShapeDtypeStruct((2 * capacity * ROW_BLK, features), bf16)

    sent = pl.pallas_call(
        lambda *refs: pack_kernel(capacity, *refs),
        out_shape=[piece] * groups,
        in_specs=[SMEM] + [VMEM] * 4,
        out_specs=[VMEM] * groups,
        name="pack",
    )(me, ret_shard, ret_block, db_keys[0], db_values[0])
    pieces = [sent[0]] + [None] * (groups - 1)
    for distance in range(groups - 1, 0, -1):
        pieces[distance] = swap(sent[distance], "dp", distance)

    row_block = jax.ShapeDtypeStruct((tokens, features), bf16)
    keys, values = pl.pallas_call(
        lambda *refs: compact_kernel(capacity, *refs),
        out_shape=[row_block] * 2,
        in_specs=[SMEM] + [VMEM] * (1 + groups),
        out_specs=[VMEM] * 2,
        name="compact",
    )(me, ret_shard, *pieces)
    key_pieces, value_pieces = [keys], [values]
    distance = columns // 2
    while distance:
        key_pieces = key_pieces + [swap(one, "ctx", distance) for one in key_pieces]
        value_pieces = value_pieces + [swap(one, "ctx", distance) for one in value_pieces]
        distance //= 2

    by_head = lambda rows: pl.BlockSpec((rows, HEAD_DIM), lambda head: (0, head))
    whole = pl.BlockSpec((count, HEAD_DIM), lambda head: (0, 0))
    context = columns * tokens
    weight_spec = pl.BlockSpec((1, count, context), lambda head: (head, 0, 0))
    acc, weights, inverse = pl.pallas_call(
        score_kernel,
        grid=(heads,),
        out_shape=[
            jax.ShapeDtypeStruct((count, features), jnp.float32),
            jax.ShapeDtypeStruct((heads, count, context), bf16),
            jax.ShapeDtypeStruct((count, HEAD_DIM), jnp.float32),
        ],
        in_specs=[SMEM] + [by_head(count)] * 3 + [by_head(tokens)] * columns,
        out_specs=[by_head(count), weight_spec, whole],
        scratch_shapes=[pltpu.VMEM((count, 2 * BLK), jnp.float32)],
        name="score",
    )(variant_blocks[0, 0], queries[0], own_keys[0], own_values[0], *key_pieces)
    attended = pl.pallas_call(
        value_kernel,
        grid=(heads,),
        out_shape=jax.ShapeDtypeStruct((count, features), bf16),
        in_specs=[by_head(count), weight_spec, whole] + [by_head(tokens)] * columns,
        out_specs=by_head(count),
        name="value",
    )(acc, weights, inverse, *value_pieces)
    return attended[None]


def solution(mesh):
    split = P("dp", "ctx", None)
    return jax.shard_map(
        per_device,
        mesh=mesh,
        in_specs=(split,) * 6 + (P(None, "ctx"),) * 2,
        out_specs=split,
        check_vma=False,
    )
```

```python
import math

import jax
import jax.numpy as jnp
from jax import lax
from jax.experimental import pallas as pl
from jax.experimental.pallas import tpu as pltpu
from jax.sharding import PartitionSpec as P

HEAD_DIM = 128
BLK = 64
ROW_BLK = 4
VAR_MOST = 2


PARAMS = pltpu.CompilerParams(vmem_limit_bytes=16 << 20)
SMEM = pl.BlockSpec(memory_space=pltpu.SMEM)
VMEM = pl.BlockSpec(memory_space=pltpu.VMEM)
masked_score = -1e30


def iota(shape, dim):
    return lax.broadcasted_iota(jnp.int32, shape, dim)


def pick(matrix, rows):
    return jnp.dot(matrix.astype(jnp.bfloat16), rows, preferred_element_type=jnp.float32).astype(
        jnp.bfloat16
    )


def pack_kernel(capacity, me_ref, shard_ref, block_ref, keys_ref, values_ref, *out_refs):
    me = me_ref[0]
    slots = shard_ref.shape[1]
    tokens = keys_ref.shape[0]
    half = capacity * ROW_BLK
    rows = jnp.concatenate([keys_ref[...], values_ref[...]], axis=0)
    row = iota((2 * half, slots), 0)
    slot = iota((2 * half, slots), 1)
    level = (row % half) // ROW_BLK
    before = (iota((slots, slots), 0) < iota((slots, slots), 1)).astype(jnp.float32)
    mine_all = (shard_ref[...] == me).astype(jnp.float32)
    earlier_all = jnp.dot(mine_all, before, preferred_element_type=jnp.float32)
    wanted_all = jnp.where(mine_all > 0, earlier_all.astype(jnp.int32), -1)
    line = iota((2 * half, 1), 0)
    base = (line // half) * tokens + line % ROW_BLK
    column = iota((2 * half, 2 * tokens), 1)
    member = iota(wanted_all.shape, 0)
    for distance, out_ref in enumerate(out_refs):
        group = me ^ distance
        here = member == group
        wanted = jnp.sum(jnp.where(here, wanted_all, 0), axis=0, keepdims=True)
        blocks = jnp.sum(jnp.where(here, block_ref[...], 0), axis=0, keepdims=True)
        source = jnp.sum(jnp.where(wanted == level, blocks, 0), axis=1, keepdims=True)
        out_ref[...] = pick(column == base + source * ROW_BLK, rows)


def compact_kernel(capacity, me_ref, shard_ref, *refs):
    piece_refs, (keys_ref, values_ref) = refs[:-2], refs[-2:]
    me = me_ref[0]
    slots = shard_ref.shape[1]
    half = capacity * ROW_BLK
    tokens = slots * ROW_BLK
    pieces = jnp.concatenate([piece_ref[...] for piece_ref in piece_refs], axis=0)
    here = iota(shard_ref.shape, 0) == me
    shards = jnp.sum(jnp.where(here, shard_ref[...], 0), axis=0, keepdims=True)
    slot = iota((tokens, slots), 0) // ROW_BLK
    lane = iota((tokens, slots), 1)
    named = jnp.sum(jnp.where(lane == slot, shards, 0), axis=1, keepdims=True)
    level = jnp.sum(((shards == named) & (lane < slot)).astype(jnp.int32), axis=1, keepdims=True)
    inside = iota((tokens, 1), 0) % ROW_BLK
    target = (named ^ me) * (2 * half) + level * ROW_BLK + inside
    column = iota((tokens, pieces.shape[0]), 1)
    keys_ref[...] = pick(column == target, pieces)
    values_ref[...] = pick(column == target + half, pieces)


def score_kernel(lengths_ref, q_ref, own_keys_ref, own_values_ref, *refs):
    key_refs, (acc_ref, weights_ref, inverse_ref, mask_ref) = refs[:-4], refs[-4:]
    head = pl.program_id(0)
    count = q_ref.shape[0]
    blocks = count // BLK
    starts = [max(0, block - 1) for block in range(blocks)]

    @pl.when(head == 0)
    def _():
        inverse_ref[...] = jnp.zeros_like(inverse_ref)
        row = iota((BLK, 2 * BLK), 0)
        column = iota((BLK, 2 * BLK), 1)
        mask_ref[0:BLK, :] = jnp.where(column <= row, 0.0, masked_score)
        for block in range(1, blocks):
            end = jnp.int32(0)
            opens = jnp.int32(0)
            for variant in range(lengths_ref.shape[0]):
                end = end + lengths_ref[variant]
                opens = opens + (end == block).astype(jnp.int32)
            first = jnp.where(opens > 0, BLK, 0)
            allowed = (column <= row + BLK) & (column >= first)
            mask_ref[block * BLK : (block + 1) * BLK, :] = jnp.where(allowed, 0.0, masked_score)

    scale = math.log2(math.e) / math.sqrt(HEAD_DIM)
    nt = (((1,), (1,)), ((), ()))
    query = q_ref[...]
    keys = jnp.concatenate([key_ref[...] for key_ref in key_refs], axis=0)
    scores = lax.dot_general(query, keys, nt, preferred_element_type=jnp.float32) * scale
    own = jnp.concatenate(
        [
            lax.dot_general(
                query[block * BLK : (block + 1) * BLK],
                own_keys_ref[starts[block] * BLK : (starts[block] + 2) * BLK, :],
                nt,
                preferred_element_type=jnp.float32,
            )
            for block in range(blocks)
        ],
        axis=0,
    )
    own = own * scale + mask_ref[...]
    largest = jnp.maximum(
        jnp.max(scores, axis=1, keepdims=True), jnp.max(own, axis=1, keepdims=True)
    )
    weights = jnp.exp2(scores - largest)
    own_weights = jnp.exp2(own - largest)
    total = jnp.sum(weights, axis=1, keepdims=True) + jnp.sum(own_weights, axis=1, keepdims=True)
    weights_ref[0] = weights.astype(jnp.bfloat16)
    own_weights = own_weights.astype(jnp.bfloat16)
    acc_ref[...] = jnp.concatenate(
        [
            jnp.dot(
                own_weights[block * BLK : (block + 1) * BLK],
                own_values_ref[starts[block] * BLK : (starts[block] + 2) * BLK, :],
                preferred_element_type=jnp.float32,
            )
            for block in range(blocks)
        ],
        axis=0,
    )
    lane = iota(inverse_ref.shape, 1)
    inverse_ref[...] = jnp.where(lane == head, 1.0 / total, inverse_ref[...])


def value_kernel(acc_ref, weights_ref, inverse_ref, *refs):
    value_refs, out_ref = refs[:-1], refs[-1]
    head = pl.program_id(0)
    values = jnp.concatenate([value_ref[...] for value_ref in value_refs], axis=0)
    lane = iota(inverse_ref.shape, 1)
    inverse = jnp.sum(jnp.where(lane == head, inverse_ref[...], 0.0), axis=1, keepdims=True)
    attended = acc_ref[...] + jnp.dot(
        weights_ref[0], values, preferred_element_type=jnp.float32
    )
    out_ref[...] = (attended * inverse).astype(out_ref.dtype)


def swap(array, axis, distance):
    size = lax.axis_size(axis)
    return lax.ppermute(array, axis, [(i, i ^ distance) for i in range(size)])


def per_device(
    queries, own_keys, own_values, variant_blocks, db_keys, db_values, ret_shard, ret_block
):
    count, features = queries.shape[1:]
    heads = features // HEAD_DIM
    groups = lax.axis_size("dp")
    columns = lax.axis_size("ctx")
    slots = ret_shard.shape[1]
    tokens = slots * ROW_BLK
    capacity = max(2, 2 * slots // groups)
    me = lax.axis_index("dp").astype(jnp.int32).reshape(1)
    bf16 = jnp.bfloat16
    piece = jax.ShapeDtypeStruct((2 * capacity * ROW_BLK, features), bf16)

    sent = pl.pallas_call(
        lambda *refs: pack_kernel(capacity, *refs),
        out_shape=[piece] * groups,
        in_specs=[SMEM] + [VMEM] * 4,
        out_specs=[VMEM] * groups,
        name="pack",
        compiler_params=PARAMS,
    )(me, ret_shard, ret_block, db_keys[0], db_values[0])
    pieces = [sent[0]] + [None] * (groups - 1)
    for distance in range(groups - 1, 0, -1):
        pieces[distance] = swap(sent[distance], "dp", distance)

    row_block = jax.ShapeDtypeStruct((tokens, features), bf16)
    keys, values = pl.pallas_call(
        lambda *refs: compact_kernel(capacity, *refs),
        out_shape=[row_block] * 2,
        in_specs=[SMEM] + [VMEM] * (1 + groups),
        out_specs=[VMEM] * 2,
        name="compact",
        compiler_params=PARAMS,
    )(me, ret_shard, *pieces)
    key_pieces, value_pieces = [keys], [values]
    distance = columns // 2
    while distance:
        key_pieces = key_pieces + [swap(one, "ctx", distance) for one in key_pieces]
        value_pieces = value_pieces + [swap(one, "ctx", distance) for one in value_pieces]
        distance //= 2

    by_head = lambda rows: pl.BlockSpec((rows, HEAD_DIM), lambda head: (0, head))
    whole = pl.BlockSpec((count, HEAD_DIM), lambda head: (0, 0))
    context = columns * tokens
    weight_spec = pl.BlockSpec((1, count, context), lambda head: (head, 0, 0))
    acc, weights, inverse = pl.pallas_call(
        score_kernel,
        grid=(heads,),
        out_shape=[
            jax.ShapeDtypeStruct((count, features), jnp.float32),
            jax.ShapeDtypeStruct((heads, count, context), bf16),
            jax.ShapeDtypeStruct((count, HEAD_DIM), jnp.float32),
        ],
        in_specs=[SMEM] + [by_head(count)] * 3 + [by_head(tokens)] * columns,
        out_specs=[by_head(count), weight_spec, whole],
        scratch_shapes=[pltpu.VMEM((count, 2 * BLK), jnp.float32)],
        name="score",
        compiler_params=PARAMS,
    )(variant_blocks[0, 0], queries[0], own_keys[0], own_values[0], *key_pieces)
    attended = pl.pallas_call(
        value_kernel,
        grid=(heads,),
        out_shape=jax.ShapeDtypeStruct((count, features), bf16),
        in_specs=[by_head(count), weight_spec, whole] + [by_head(tokens)] * columns,
        out_specs=by_head(count),
        name="value",
        compiler_params=PARAMS,
    )(acc, weights, inverse, *value_pieces)
    return attended[None]


def solution(mesh):
    split = P("dp", "ctx", None)
    return jax.shard_map(
        per_device,
        mesh=mesh,
        in_specs=(split,) * 6 + (P(None, "ctx"),) * 2,
        out_specs=split,
        check_vma=False,
    )
```

```python
import math

import jax
import jax.numpy as jnp
from jax import lax
from jax.experimental import pallas as pl
from jax.experimental.pallas import tpu as pltpu
from jax.sharding import PartitionSpec as P

HEAD_DIM = 128
BLK = 64
ROW_BLK = 4
VAR_MOST = 2


PARAMS = pltpu.CompilerParams(vmem_limit_bytes=16 << 20)
SMEM = pl.BlockSpec(memory_space=pltpu.SMEM)
VMEM = pl.BlockSpec(memory_space=pltpu.VMEM)
HBM = pl.BlockSpec(memory_space=pltpu.HBM)
SCALE = math.log2(math.e) / math.sqrt(HEAD_DIM)
NT = (((1,), (1,)), ((), ()))
ROWS = 128
masked_score = -1e30


def iota(shape, dim):
    return lax.broadcasted_iota(jnp.int32, shape, dim)


def pick(matrix, rows):
    return jnp.dot(matrix.astype(jnp.bfloat16), rows, preferred_element_type=jnp.float32).astype(
        jnp.bfloat16
    )


def pack_kernel(capacity, me_ref, shard_hbm, block_hbm, keys_hbm, values_hbm, *refs):
    out_refs, (shard_ref, block_ref, rows_ref, sems) = refs[:-4], refs[-4:]
    me = me_ref[0]
    slots = shard_ref.shape[1]
    tokens = keys_hbm.shape[0]
    half = capacity * ROW_BLK
    copies = [
        pltpu.make_async_copy(source, target, sems.at[number])
        for number, (source, target) in enumerate(
            (
                (shard_hbm, shard_ref),
                (block_hbm, block_ref),
                (keys_hbm, rows_ref.at[0:tokens]),
                (values_hbm, rows_ref.at[tokens : 2 * tokens]),
            )
        )
    ]
    for copy in copies:
        copy.start()
    for copy in copies:
        copy.wait()
    rows = rows_ref[...]
    row = iota((2 * half, slots), 0)
    level = (row % half) // ROW_BLK
    before = (iota((slots, slots), 0) < iota((slots, slots), 1)).astype(jnp.float32)
    mine_all = (shard_ref[...] == me).astype(jnp.float32)
    earlier_all = jnp.dot(mine_all, before, preferred_element_type=jnp.float32)
    wanted_all = jnp.where(mine_all > 0, earlier_all.astype(jnp.int32), -1)
    line = iota((2 * half, 1), 0)
    base = (line // half) * tokens + line % ROW_BLK
    column = iota((2 * half, 2 * tokens), 1)
    member = iota(wanted_all.shape, 0)
    for distance, out_ref in enumerate(out_refs):
        group = me ^ distance
        here = member == group
        wanted = jnp.sum(jnp.where(here, wanted_all, 0), axis=0, keepdims=True)
        blocks = jnp.sum(jnp.where(here, block_ref[...], 0), axis=0, keepdims=True)
        source = jnp.sum(jnp.where(wanted == level, blocks, 0), axis=1, keepdims=True)
        out_ref[...] = pick(column == base + source * ROW_BLK, rows)


def compact_kernel(capacity, me_ref, shard_ref, after_ref, *refs):
    piece_refs, (keys_ref, values_ref) = refs[:-2], refs[-2:]
    me = me_ref[0]
    slots = shard_ref.shape[1]
    half = capacity * ROW_BLK
    tokens = slots * ROW_BLK
    pieces = jnp.concatenate([piece_ref[...] for piece_ref in piece_refs], axis=0)
    here = iota(shard_ref.shape, 0) == me
    shards = jnp.sum(jnp.where(here, shard_ref[...], 0), axis=0, keepdims=True)
    slot = iota((tokens, slots), 0) // ROW_BLK
    lane = iota((tokens, slots), 1)
    named = jnp.sum(jnp.where(lane == slot, shards, 0), axis=1, keepdims=True)
    level = jnp.sum(((shards == named) & (lane < slot)).astype(jnp.int32), axis=1, keepdims=True)
    inside = iota((tokens, 1), 0) % ROW_BLK
    target = (named ^ me) * (2 * half) + level * ROW_BLK + inside
    column = iota((tokens, pieces.shape[0]), 1)
    keys_ref[...] = pick(column == target, pieces)
    values_ref[...] = pick(column == target + half, pieces)


def own_kernel(
    lengths_ref,
    q_hbm,
    keys_hbm,
    values_hbm,
    after_ref,
    query_ref,
    acc_ref,
    largest_ref,
    total_ref,
    mask_ref,
    keys_ref,
    values_ref,
    sems,
):
    copies = [
        pltpu.make_async_copy(source, target, sems.at[number])
        for number, (source, target) in enumerate(
            ((q_hbm, query_ref), (keys_hbm, keys_ref), (values_hbm, values_ref))
        )
    ]
    for copy in copies:
        copy.start()
    count, features = query_ref.shape
    blocks = count // BLK
    starts = [max(0, block - 1) * BLK for block in range(blocks)]
    row = iota((BLK, 2 * BLK), 0)
    column = iota((BLK, 2 * BLK), 1)
    mask_ref[0:BLK, :] = jnp.where(column <= row, 0.0, masked_score)
    for block in range(1, blocks):
        end = jnp.int32(0)
        opens = jnp.int32(0)
        for variant in range(lengths_ref.shape[0]):
            end = end + lengths_ref[variant]
            opens = opens + (end == block).astype(jnp.int32)
        first = jnp.where(opens > 0, BLK, 0)
        allowed = (column <= row + BLK) & (column >= first)
        mask_ref[block * BLK : (block + 1) * BLK, :] = jnp.where(allowed, 0.0, masked_score)
    for copy in copies:
        copy.wait()
    for head in range(features // HEAD_DIM):
        lanes = slice(head * HEAD_DIM, (head + 1) * HEAD_DIM)
        for block in range(blocks):
            rows = slice(block * BLK, (block + 1) * BLK)
            band = slice(starts[block], starts[block] + 2 * BLK)
            scores = lax.dot_general(
                query_ref[rows, lanes], keys_ref[band, lanes], NT, preferred_element_type=jnp.float32
            )
            scores = scores * SCALE + mask_ref[rows, :]
            largest = jnp.max(scores, axis=1, keepdims=True)
            weights = jnp.exp2(scores - largest)
            total = jnp.sum(weights, axis=1, keepdims=True)
            acc_ref[rows, lanes] = jnp.dot(
                weights.astype(jnp.bfloat16),
                values_ref[band, lanes],
                preferred_element_type=jnp.float32,
            )
            largest_ref[rows, lanes] = jnp.broadcast_to(largest, (BLK, HEAD_DIM))
            total_ref[rows, lanes] = jnp.broadcast_to(total, (BLK, HEAD_DIM))


def score_kernel(query_ref, acc_ref, largest_ref, total_ref, *refs):
    key_refs, (weights_ref, scaled_ref, inverse_ref) = refs[:-3], refs[-3:]
    count, features = query_ref.shape
    for head in range(features // HEAD_DIM):
        lanes = slice(head * HEAD_DIM, (head + 1) * HEAD_DIM)
        keys = jnp.concatenate([key_ref[:, lanes] for key_ref in key_refs], axis=0)
        for start in range(0, count, ROWS):
            rows = slice(start, start + ROWS)
            scores = lax.dot_general(
                query_ref[rows, lanes], keys, NT, preferred_element_type=jnp.float32
            )
            scores = scores * SCALE
            own = largest_ref[rows, lanes]
            largest = jnp.maximum(own, jnp.max(scores, axis=1, keepdims=True))
            weights = jnp.exp2(scores - largest[:, :1])
            rescale = jnp.exp2(own - largest)
            total = total_ref[rows, lanes] * rescale + jnp.sum(weights, axis=1, keepdims=True)
            weights_ref[head, rows, :] = weights.astype(jnp.bfloat16)
            scaled_ref[rows, lanes] = acc_ref[rows, lanes] * rescale
            inverse_ref[rows, lanes] = 1.0 / total


def value_kernel(scaled_ref, weights_ref, inverse_ref, *refs):
    value_refs, (out_hbm, out_ref, sems) = refs[:-3], refs[-3:]
    count, features = scaled_ref.shape
    copies = []
    for head in range(features // HEAD_DIM):
        lanes = slice(head * HEAD_DIM, (head + 1) * HEAD_DIM)
        values = jnp.concatenate([value_ref[:, lanes] for value_ref in value_refs], axis=0)
        attended = scaled_ref[:, lanes] + jnp.dot(
            weights_ref[head], values, preferred_element_type=jnp.float32
        )
        out_ref[:, lanes] = (attended * inverse_ref[:, lanes]).astype(out_ref.dtype)
        copies.append(
            pltpu.make_async_copy(out_ref.at[:, lanes], out_hbm.at[:, lanes], sems.at[head])
        )
        copies[-1].start()
    for copy in copies:
        copy.wait()


def hbm(array):
    return pltpu.with_memory_space_constraint(array, pltpu.HBM)


def swap(array, axis, distance):
    size = lax.axis_size(axis)
    return lax.ppermute(array, axis, [(i, i ^ distance) for i in range(size)])


def per_device(
    queries, own_keys, own_values, variant_blocks, db_keys, db_values, ret_shard, ret_block
):
    count, features = queries.shape[1:]
    heads = features // HEAD_DIM
    groups = lax.axis_size("dp")
    columns = lax.axis_size("ctx")
    slots = ret_shard.shape[1]
    tokens = slots * ROW_BLK
    capacity = max(2, 2 * slots // groups)
    me = lax.axis_index("dp").astype(jnp.int32).reshape(1)
    bf16 = jnp.bfloat16
    context = columns * tokens
    wide = jax.ShapeDtypeStruct((count, features), jnp.float32)
    piece = jax.ShapeDtypeStruct((2 * capacity * ROW_BLK, features), bf16)

    sent = pl.pallas_call(
        lambda *refs: pack_kernel(capacity, *refs),
        out_shape=[piece] * groups,
        in_specs=[SMEM] + [HBM] * 4,
        out_specs=[VMEM] * groups,
        scratch_shapes=[
            pltpu.VMEM(ret_shard.shape, jnp.int32),
            pltpu.VMEM(ret_block.shape, jnp.int32),
            pltpu.VMEM((2 * tokens, features), bf16),
            pltpu.SemaphoreType.DMA((4,)),
        ],
        name="pack",
        compiler_params=PARAMS,
    )(me, hbm(ret_shard), hbm(ret_block), hbm(db_keys[0]), hbm(db_values[0]))
    pieces = [sent[0]] + [None] * (groups - 1)
    for distance in range(groups - 1, 0, -1):
        pieces[distance] = swap(sent[distance], "dp", distance)

    query, acc, largest, total = pl.pallas_call(
        own_kernel,
        out_shape=[jax.ShapeDtypeStruct((count, features), bf16)] + [wide] * 3,
        in_specs=[SMEM] + [HBM] * 3 + [VMEM],
        out_specs=[VMEM] * 4,
        scratch_shapes=[
            pltpu.VMEM((count, 2 * BLK), jnp.float32),
            pltpu.VMEM((count, features), bf16),
            pltpu.VMEM((count, features), bf16),
            pltpu.SemaphoreType.DMA((3,)),
        ],
        name="own",
        compiler_params=PARAMS,
        cost_estimate=pl.CostEstimate(
            flops=4 * count * 2 * BLK * features,
            transcendentals=2 * count * BLK * heads,
            bytes_accessed=20 * count * features,
        ),
    )(variant_blocks[0, 0], hbm(queries[0]), hbm(own_keys[0]), hbm(own_values[0]), sent[0])
    row_block = jax.ShapeDtypeStruct((tokens, features), bf16)
    keys, values = pl.pallas_call(
        lambda *refs: compact_kernel(capacity, *refs),
        out_shape=[row_block] * 2,
        in_specs=[SMEM] + [VMEM] * (2 + groups),
        out_specs=[VMEM] * 2,
        name="compact",
        compiler_params=PARAMS,
    )(me, ret_shard, total, *pieces)
    key_pieces, value_pieces = [keys], [values]
    distance = columns // 2
    while distance:
        key_pieces = key_pieces + [swap(one, "ctx", distance) for one in key_pieces]
        value_pieces = value_pieces + [swap(one, "ctx", distance) for one in value_pieces]
        distance //= 2

    weights, scaled, inverse = pl.pallas_call(
        score_kernel,
        out_shape=[jax.ShapeDtypeStruct((heads, count, context), bf16), wide, wide],
        in_specs=[VMEM] * (4 + columns),
        out_specs=[VMEM] * 3,
        name="score",
        compiler_params=PARAMS,
    )(query, acc, largest, total, *key_pieces)
    attended = pl.pallas_call(
        value_kernel,
        out_shape=jax.ShapeDtypeStruct((count, features), bf16),
        in_specs=[VMEM] * (3 + columns),
        out_specs=HBM,
        scratch_shapes=[
            pltpu.VMEM((count, features), bf16),
            pltpu.SemaphoreType.DMA((heads,)),
        ],
        name="value",
        compiler_params=PARAMS,
    )(scaled, weights, inverse, *value_pieces)
    return attended[None]


def solution(mesh):
    split = P("dp", "ctx", None)
    return jax.shard_map(
        per_device,
        mesh=mesh,
        in_specs=(split,) * 6 + (P(None, "ctx"),) * 2,
        out_specs=split,
        check_vma=False,
    )
```

```python
import functools
import math

import jax
import jax.numpy as jnp
from jax import lax
from jax.experimental import pallas as pl
from jax.experimental.pallas import tpu as pltpu
from jax.sharding import PartitionSpec as P


HEAD_DIM = 128
BLK = 64
ROW_BLK = 4


PARAMS = pltpu.CompilerParams(vmem_limit_bytes=16 << 20)
SMEM = pl.BlockSpec(memory_space=pltpu.SMEM)
VMEM = pl.BlockSpec(memory_space=pltpu.VMEM)
HBM = pl.BlockSpec(memory_space=pltpu.HBM)
SCALE = math.log2(math.e) / math.sqrt(HEAD_DIM)
NT = (((1,), (1,)), ((), ()))
masked_score = -1e30


def iota(shape, dim):
    return lax.broadcasted_iota(jnp.int32, shape, dim)


def pick(matrix, rows):
    return jnp.dot(matrix.astype(jnp.bfloat16), rows, preferred_element_type=jnp.float32).astype(
        jnp.bfloat16
    )


def pack_kernel(capacity, me_ref, shard_hbm, block_hbm, keys_hbm, values_hbm, *refs):
    out_refs, (shard_ref, block_ref, rows_ref, sems) = refs[:-4], refs[-4:]
    me = me_ref[0]
    slots = shard_ref.shape[1]
    tokens = keys_hbm.shape[0]
    half = capacity * ROW_BLK
    copies = [
        pltpu.make_async_copy(source, target, sems.at[number])
        for number, (source, target) in enumerate(
            (
                (shard_hbm, shard_ref),
                (block_hbm, block_ref),
                (keys_hbm, rows_ref.at[0:tokens]),
                (values_hbm, rows_ref.at[tokens : 2 * tokens]),
            )
        )
    ]
    for copy in copies:
        copy.start()
    for copy in copies:
        copy.wait()
    rows = rows_ref[...]
    row = iota((2 * half, slots), 0)
    level = (row % half) // ROW_BLK
    before = (iota((slots, slots), 0) < iota((slots, slots), 1)).astype(jnp.float32)
    mine_all = (shard_ref[...] == me).astype(jnp.float32)
    earlier_all = jnp.dot(mine_all, before, preferred_element_type=jnp.float32)
    wanted_all = jnp.where(mine_all > 0, earlier_all.astype(jnp.int32), -1)
    line = iota((2 * half, 1), 0)
    base = (line // half) * tokens + line % ROW_BLK
    column = iota((2 * half, 2 * tokens), 1)
    member = iota(wanted_all.shape, 0)
    for distance, out_ref in enumerate(out_refs):
        group = me ^ distance
        here = member == group
        wanted = jnp.sum(jnp.where(here, wanted_all, 0), axis=0, keepdims=True)
        blocks = jnp.sum(jnp.where(here, block_ref[...], 0), axis=0, keepdims=True)
        source = jnp.sum(jnp.where(wanted == level, blocks, 0), axis=1, keepdims=True)
        out_ref[...] = pick(column == base + source * ROW_BLK, rows)


def compact_kernel(capacity, me_ref, shard_ref, after_ref, *refs):
    piece_refs, (keys_ref, values_ref) = refs[:-2], refs[-2:]
    me = me_ref[0]
    slots = shard_ref.shape[1]
    half = capacity * ROW_BLK
    tokens = slots * ROW_BLK
    pieces = jnp.concatenate([piece_ref[...] for piece_ref in piece_refs], axis=0)
    here = iota(shard_ref.shape, 0) == me
    shards = jnp.sum(jnp.where(here, shard_ref[...], 0), axis=0, keepdims=True)
    slot = iota((tokens, slots), 0) // ROW_BLK
    lane = iota((tokens, slots), 1)
    named = jnp.sum(jnp.where(lane == slot, shards, 0), axis=1, keepdims=True)
    level = jnp.sum(((shards == named) & (lane < slot)).astype(jnp.int32), axis=1, keepdims=True)
    inside = iota((tokens, 1), 0) % ROW_BLK
    target = (named ^ me) * (2 * half) + level * ROW_BLK + inside
    column = iota((tokens, pieces.shape[0]), 1)
    keys_ref[...] = pick(column == target, pieces)
    values_ref[...] = pick(column == target + half, pieces)


def weigh(weights, values):
    both = jnp.concatenate([values, jnp.ones_like(values)], axis=1)
    result = jnp.dot(weights, both, preferred_element_type=jnp.float32)
    return result[:, :HEAD_DIM], result[:, HEAD_DIM:]


def own_kernel(
    lengths_ref,
    q_hbm,
    keys_hbm,
    values_hbm,
    after_ref,
    query_ref,
    acc_ref,
    largest_ref,
    total_ref,
    mask_ref,
    keys_ref,
    values_ref,
    weights_ref,
    sems,
):
    copies = [
        pltpu.make_async_copy(source, target, sems.at[number])
        for number, (source, target) in enumerate(
            ((q_hbm, query_ref), (keys_hbm, keys_ref), (values_hbm, values_ref))
        )
    ]
    for copy in copies:
        copy.start()
    count, features = query_ref.shape
    blocks = count // BLK
    starts = [max(0, block - 1) * BLK for block in range(blocks)]
    row = iota((BLK, 2 * BLK), 0)
    column = iota((BLK, 2 * BLK), 1)
    mask_ref[0:BLK, :] = jnp.where(column <= row, 0.0, masked_score)
    for block in range(1, blocks):
        end = jnp.int32(0)
        opens = jnp.int32(0)
        for variant in range(lengths_ref.shape[0]):
            end = end + lengths_ref[variant]
            opens = opens + (end == block).astype(jnp.int32)
        first = jnp.where(opens > 0, BLK, 0)
        allowed = (column <= row + BLK) & (column >= first)
        mask_ref[block * BLK : (block + 1) * BLK, :] = jnp.where(allowed, 0.0, masked_score)
    for copy in copies:
        copy.wait()
    for head in range(features // HEAD_DIM):
        lanes = slice(head * HEAD_DIM, (head + 1) * HEAD_DIM)
        for block in range(blocks):
            rows = slice(block * BLK, (block + 1) * BLK)
            acc_ref[rows, lanes] = lax.dot_general(
                query_ref[rows, lanes],
                keys_ref[starts[block] : starts[block] + 2 * BLK, lanes],
                NT,
                preferred_element_type=jnp.float32,
            )
    for head in range(features // HEAD_DIM):
        lanes = slice(head * HEAD_DIM, (head + 1) * HEAD_DIM)
        scores = acc_ref[:, lanes] * SCALE + mask_ref[...]
        largest = jnp.max(scores, axis=1, keepdims=True)
        weights = jnp.exp2(scores - largest)
        weights_ref[:, lanes] = weights.astype(jnp.bfloat16)
        largest_ref[:, lanes] = jnp.broadcast_to(largest, (count, HEAD_DIM))
    for head in range(features // HEAD_DIM):
        lanes = slice(head * HEAD_DIM, (head + 1) * HEAD_DIM)
        for block in range(blocks):
            rows = slice(block * BLK, (block + 1) * BLK)
            acc_ref[rows, lanes], total_ref[rows, lanes] = weigh(
                weights_ref[rows, lanes], values_ref[starts[block] : starts[block] + 2 * BLK, lanes]
            )


LAZY = 60.0


def context_kernel(last, query_ref, acc_ref, largest_ref, total_ref, *refs):
    out_count = 4 if last else 3
    refs, out_refs = refs[:-out_count], refs[-out_count:]
    if last:
        key_refs, value_refs = refs, None
        weights_ref, new_acc_ref, new_largest_ref, inverse_ref = out_refs
    else:
        key_refs, value_refs = refs[: len(refs) // 2], refs[len(refs) // 2 :]
        new_acc_ref, new_largest_ref, new_total_ref = out_refs
    features = query_ref.shape[1]

    def absorb(exact):
        excess = None
        for head in range(features // HEAD_DIM):
            lanes = slice(head * HEAD_DIM, (head + 1) * HEAD_DIM)
            keys = jnp.concatenate([key_ref[:, lanes] for key_ref in key_refs], axis=0)
            scores = lax.dot_general(
                query_ref[:, lanes], keys, NT, preferred_element_type=jnp.float32
            )
            scores = scores * SCALE
            largest = new_largest_ref[:, lanes]
            acc, total = (new_acc_ref if last else acc_ref)[:, lanes], total_ref[:, lanes]
            if exact:
                before = largest
                largest = jnp.maximum(before, jnp.max(scores, axis=1, keepdims=True))
                rescale = jnp.exp2(before - largest)
                acc, total = acc * rescale, total * rescale
                new_largest_ref[:, lanes] = largest
            scores = scores - largest[:, :1]
            if not exact:
                highest = functools.reduce(
                    jnp.maximum,
                    [scores[start : start + BLK] for start in range(0, scores.shape[0], BLK)],
                )
                excess = highest if excess is None else jnp.maximum(excess, highest)
            weights = jnp.exp2(scores).astype(jnp.bfloat16)
            if last:
                weights_ref[head] = weights
                ones = jnp.ones((keys.shape[0], HEAD_DIM), weights.dtype)
                more = jnp.dot(weights, ones, preferred_element_type=jnp.float32)
                inverse_ref[:, lanes] = 1.0 / (total + more)
                if exact:
                    new_acc_ref[:, lanes] = acc
            else:
                values = jnp.concatenate([value_ref[:, lanes] for value_ref in value_refs], axis=0)
                more_acc, more = weigh(weights, values)
                new_acc_ref[:, lanes] = acc + more_acc
                new_total_ref[:, lanes] = total + more
        return excess

    excess = jnp.max(absorb(False))

    @pl.when(excess > LAZY)
    def _():
        absorb(True)


def value_kernel(scaled_ref, weights_ref, inverse_ref, *refs):
    value_refs, (out_hbm, out_ref, sems) = refs[:-3], refs[-3:]
    _, features = scaled_ref.shape
    copies = []
    for head in range(features // HEAD_DIM):
        lanes = slice(head * HEAD_DIM, (head + 1) * HEAD_DIM)
        values = jnp.concatenate([value_ref[:, lanes] for value_ref in value_refs], axis=0)
        attended = scaled_ref[:, lanes] + jnp.dot(
            weights_ref[head], values, preferred_element_type=jnp.float32
        )
        out_ref[:, lanes] = (attended * inverse_ref[:, lanes]).astype(out_ref.dtype)
        copies.append(
            pltpu.make_async_copy(out_ref.at[:, lanes], out_hbm.at[:, lanes], sems.at[head])
        )
        copies[-1].start()
    for copy in copies:
        copy.wait()


def hbm(array):
    return pltpu.with_memory_space_constraint(array, pltpu.HBM)


def swap(array, axis, distance):
    size = lax.axis_size(axis)
    return lax.ppermute(array, axis, [(i, i ^ distance) for i in range(size)])


def gather_pair(keys, values):
    return (keys, values), (swap(keys, "ctx", 1), swap(values, "ctx", 1))


def per_device(
    queries, own_keys, own_values, variant_blocks, db_keys, db_values, ret_shard, ret_block
):
    count, features = queries.shape[1:]
    heads = features // HEAD_DIM
    groups = lax.axis_size("dp")
    columns = lax.axis_size("ctx")
    slots = ret_shard.shape[1]
    tokens = slots * ROW_BLK
    capacity = max(2, 2 * slots // groups)
    me = lax.axis_index("dp").astype(jnp.int32).reshape(1)
    bf16 = jnp.bfloat16
    wide = jax.ShapeDtypeStruct((count, features), jnp.float32)
    piece = jax.ShapeDtypeStruct((2 * capacity * ROW_BLK, features), bf16)

    sent = pl.pallas_call(
        lambda *refs: pack_kernel(capacity, *refs),
        out_shape=[piece] * groups,
        in_specs=[SMEM] + [HBM] * 4,
        out_specs=[VMEM] * groups,
        scratch_shapes=[
            pltpu.VMEM(ret_shard.shape, jnp.int32),
            pltpu.VMEM(ret_block.shape, jnp.int32),
            pltpu.VMEM((2 * tokens, features), bf16),
            pltpu.SemaphoreType.DMA((4,)),
        ],
        name="pack",
        compiler_params=PARAMS,
    )(me, hbm(ret_shard), hbm(ret_block), hbm(db_keys[0]), hbm(db_values[0]))
    pieces = [sent[0]]
    for distance in range(1, groups):
        pieces.append(swap(sent[distance], "dp", distance))
    query, acc, largest, total = pl.pallas_call(
        own_kernel,
        out_shape=[jax.ShapeDtypeStruct((count, features), bf16)] + [wide] * 3,
        in_specs=[SMEM] + [HBM] * 3 + [VMEM],
        out_specs=[VMEM] * 4,
        scratch_shapes=[
            pltpu.VMEM((count, 2 * BLK), jnp.float32),
            pltpu.VMEM((count, features), bf16),
            pltpu.VMEM((count, features), bf16),
            pltpu.VMEM((count, features), bf16),
            pltpu.SemaphoreType.DMA((3,)),
        ],
        name="own",
        compiler_params=PARAMS,
        cost_estimate=pl.CostEstimate(
            flops=4 * count * 2 * BLK * features,
            transcendentals=2 * count * BLK * heads,
            bytes_accessed=20 * count * features,
        ),
    )(variant_blocks[0, 0], hbm(queries[0]), hbm(own_keys[0]), hbm(own_values[0]), sent[0])
    row_block = jax.ShapeDtypeStruct((tokens, features), bf16)
    keys, values = pl.pallas_call(
        lambda *refs: compact_kernel(capacity, *refs),
        out_shape=[row_block] * 2,
        in_specs=[SMEM] + [VMEM] * (2 + groups),
        out_specs=[VMEM] * 2,
        name="compact",
        compiler_params=PARAMS,
    )(me, ret_shard, total, *pieces)
    far = []
    distance = columns // 2
    while distance > 1:
        far_keys = [swap(one, "ctx", distance) for one in [keys] + [k for k, _ in far]]
        far_values = [swap(one, "ctx", distance) for one in [values] + [v for _, v in far]]
        far = far + list(zip(far_keys, far_values))
        distance //= 2
    near = gather_pair(keys, values)
    far = [pair for one in far for pair in gather_pair(*one)]
    acc, largest, total = pl.pallas_call(
        lambda *refs: context_kernel(False, *refs),
        out_shape=[wide] * 3,
        in_specs=[VMEM] * (4 + 2 * len(near)),
        out_specs=[VMEM] * 3,
        input_output_aliases={2: 1},
        name="near",
        compiler_params=PARAMS,
    )(query, acc, largest, total, *[k for k, _ in near], *[v for _, v in near])
    weights, acc, largest, inverse = pl.pallas_call(
        lambda *refs: context_kernel(True, *refs),
        out_shape=[jax.ShapeDtypeStruct((heads, count, len(far) * tokens), bf16)] + [wide] * 3,
        in_specs=[VMEM] * (4 + len(far)),
        out_specs=[VMEM] * 4,
        input_output_aliases={1: 1, 2: 2},
        name="score",
        compiler_params=PARAMS,
    )(query, acc, largest, total, *[k for k, _ in far])
    attended = pl.pallas_call(
        value_kernel,
        out_shape=jax.ShapeDtypeStruct((count, features), bf16),
        in_specs=[VMEM] * (3 + len(far)),
        out_specs=HBM,
        scratch_shapes=[
            pltpu.VMEM((count, features), bf16),
            pltpu.SemaphoreType.DMA((heads,)),
        ],
        name="value",
        compiler_params=PARAMS,
    )(acc, weights, inverse, *[v for _, v in far])
    return attended[None]


def solution(mesh):
    split = P("dp", "ctx", None)
    return jax.shard_map(
        per_device,
        mesh=mesh,
        in_specs=(split,) * 6 + (P(None, "ctx"),) * 2,
        out_specs=split,
        check_vma=False,
    )
```

```python
import functools
import math

import jax
import jax.numpy as jnp
from jax import lax
from jax.experimental import pallas as pl
from jax.experimental.pallas import tpu as pltpu
from jax.sharding import PartitionSpec as P


HEAD_DIM = 128
BLK = 64
ROW_BLK = 4


PARAMS = pltpu.CompilerParams(vmem_limit_bytes=16 << 20)
SMEM = pl.BlockSpec(memory_space=pltpu.SMEM)
VMEM = pl.BlockSpec(memory_space=pltpu.VMEM)
HBM = pl.BlockSpec(memory_space=pltpu.HBM)
SCALE = math.log2(math.e) / math.sqrt(HEAD_DIM)
NT = (((1,), (1,)), ((), ()))
masked_score = -1e30


def iota(shape, dim):
    return lax.broadcasted_iota(jnp.int32, shape, dim)


def pick(matrix, rows):
    return jnp.dot(matrix.astype(jnp.bfloat16), rows, preferred_element_type=jnp.float32).astype(
        jnp.bfloat16
    )


def pack_kernel(capacity, me_ref, shard_hbm, block_hbm, keys_hbm, values_hbm, *refs):
    out_refs, (shard_ref, block_ref, rows_ref, sems) = refs[:-4], refs[-4:]
    me = me_ref[0]
    slots = shard_ref.shape[1]
    tokens = keys_hbm.shape[0]
    half = capacity * ROW_BLK
    copies = [
        pltpu.make_async_copy(source, target, sems.at[number])
        for number, (source, target) in enumerate(
            (
                (shard_hbm, shard_ref),
                (block_hbm, block_ref),
                (keys_hbm, rows_ref.at[0:tokens]),
                (values_hbm, rows_ref.at[tokens : 2 * tokens]),
            )
        )
    ]
    for copy in copies:
        copy.start()
    for copy in copies[:2]:
        copy.wait()
    row = iota((2 * half, slots), 0)
    level = (row % half) // ROW_BLK
    before = (iota((slots, slots), 0) < iota((slots, slots), 1)).astype(jnp.float32)
    mine_all = (shard_ref[...] == me).astype(jnp.float32)
    earlier_all = jnp.dot(mine_all, before, preferred_element_type=jnp.float32)
    wanted_all = jnp.where(mine_all > 0, earlier_all.astype(jnp.int32), -1)
    line = iota((2 * half, 1), 0)
    base = (line // half) * tokens + line % ROW_BLK
    column = iota((2 * half, 2 * tokens), 1)
    member = iota(wanted_all.shape, 0)
    choices = []
    for distance in range(len(out_refs)):
        here = member == (me ^ distance)
        wanted = jnp.sum(jnp.where(here, wanted_all, 0), axis=0, keepdims=True)
        blocks = jnp.sum(jnp.where(here, block_ref[...], 0), axis=0, keepdims=True)
        source = jnp.sum(jnp.where(wanted == level, blocks, 0), axis=1, keepdims=True)
        choices.append((column == base + source * ROW_BLK).astype(jnp.bfloat16))
    choice = jnp.concatenate(choices, axis=0)
    for copy in copies[2:]:
        copy.wait()
    picked = pick(choice, rows_ref[...])
    for distance, out_ref in enumerate(out_refs):
        out_ref[...] = picked[distance * 2 * half : (distance + 1) * 2 * half]


def context_choice(capacity, me, shards_all, piece_rows):
    slots = shards_all.shape[1]
    half = capacity * ROW_BLK
    tokens = slots * ROW_BLK
    here = iota(shards_all.shape, 0) == me
    shards = jnp.sum(jnp.where(here, shards_all, 0), axis=0, keepdims=True)
    line = iota((2 * tokens, slots), 0)
    slot = (line % tokens) // ROW_BLK
    lane = iota((2 * tokens, slots), 1)
    named = jnp.sum(jnp.where(lane == slot, shards, 0), axis=1, keepdims=True)
    level = jnp.sum(((shards == named) & (lane < slot)).astype(jnp.int32), axis=1, keepdims=True)
    line = line[:, :1]
    inside = line % ROW_BLK + (line // tokens) * half
    target = (named ^ me) * (2 * half) + level * ROW_BLK + inside
    return (iota((2 * tokens, piece_rows), 1) == target).astype(jnp.bfloat16)


def compact_kernel(choice_ref, *refs):
    piece_refs, (keys_ref, values_ref) = refs[:-2], refs[-2:]
    pieces = jnp.concatenate([piece_ref[...] for piece_ref in piece_refs], axis=0)
    picked = pick(choice_ref[...], pieces)
    keys_ref[...] = picked[: keys_ref.shape[0]]
    values_ref[...] = picked[keys_ref.shape[0] :]


def weigh(weights, values):
    both = jnp.concatenate([values, jnp.ones_like(values)], axis=1)
    result = jnp.dot(weights, both, preferred_element_type=jnp.float32)
    return result[:, :HEAD_DIM], result[:, HEAD_DIM:]


def own_kernel(
    capacity,
    me_ref,
    lengths_ref,
    shard_ref,
    q_hbm,
    keys_hbm,
    values_hbm,
    after_ref,
    query_ref,
    acc_ref,
    largest_ref,
    total_ref,
    choice_ref,
    mask_ref,
    keys_ref,
    values_ref,
    weights_ref,
    sems,
):
    copies = [
        pltpu.make_async_copy(source, target, sems.at[number])
        for number, (source, target) in enumerate(
            ((q_hbm, query_ref), (keys_hbm, keys_ref), (values_hbm, values_ref))
        )
    ]
    for copy in copies:
        copy.start()
    choice_ref[...] = context_choice(capacity, me_ref[0], shard_ref[...], choice_ref.shape[1])
    count, features = query_ref.shape
    blocks = count // BLK
    starts = [max(0, block - 1) * BLK for block in range(blocks)]
    row = iota((BLK, 2 * BLK), 0)
    column = iota((BLK, 2 * BLK), 1)
    mask_ref[0:BLK, :] = jnp.where(column <= row, 0.0, masked_score)
    for block in range(1, blocks):
        end = jnp.int32(0)
        opens = jnp.int32(0)
        for variant in range(lengths_ref.shape[0]):
            end = end + lengths_ref[variant]
            opens = opens + (end == block).astype(jnp.int32)
        first = jnp.where(opens > 0, BLK, 0)
        allowed = (column <= row + BLK) & (column >= first)
        mask_ref[block * BLK : (block + 1) * BLK, :] = jnp.where(allowed, 0.0, masked_score)
    for copy in copies:
        copy.wait()
    for head in range(features // HEAD_DIM):
        lanes = slice(head * HEAD_DIM, (head + 1) * HEAD_DIM)
        for block in range(blocks):
            rows = slice(block * BLK, (block + 1) * BLK)
            acc_ref[rows, lanes] = lax.dot_general(
                query_ref[rows, lanes],
                keys_ref[starts[block] : starts[block] + 2 * BLK, lanes],
                NT,
                preferred_element_type=jnp.float32,
            )
    for head in range(features // HEAD_DIM):
        lanes = slice(head * HEAD_DIM, (head + 1) * HEAD_DIM)
        scores = acc_ref[:, lanes] * SCALE + mask_ref[...]
        largest = jnp.max(scores, axis=1, keepdims=True)
        weights = jnp.exp2(scores - largest)
        weights_ref[:, lanes] = weights.astype(jnp.bfloat16)
        largest_ref[:, lanes] = jnp.broadcast_to(largest, (count, HEAD_DIM))
    for head in range(features // HEAD_DIM):
        lanes = slice(head * HEAD_DIM, (head + 1) * HEAD_DIM)
        for block in range(blocks):
            rows = slice(block * BLK, (block + 1) * BLK)
            acc_ref[rows, lanes], total_ref[rows, lanes] = weigh(
                weights_ref[rows, lanes], values_ref[starts[block] : starts[block] + 2 * BLK, lanes]
            )


LAZY = 60.0


def context_kernel(last, query_ref, acc_ref, largest_ref, total_ref, *refs):
    out_count = 4 if last else 3
    refs, out_refs = refs[:-out_count], refs[-out_count:]
    if last:
        key_refs, value_refs = refs, None
        weights_ref, new_acc_ref, new_largest_ref, inverse_ref = out_refs
    else:
        key_refs, value_refs = refs[: len(refs) // 2], refs[len(refs) // 2 :]
        new_acc_ref, new_largest_ref, new_total_ref = out_refs
    features = query_ref.shape[1]

    def absorb(exact):
        excess = None
        for head in range(features // HEAD_DIM):
            lanes = slice(head * HEAD_DIM, (head + 1) * HEAD_DIM)
            keys = jnp.concatenate([key_ref[:, lanes] for key_ref in key_refs], axis=0)
            scores = lax.dot_general(
                query_ref[:, lanes], keys, NT, preferred_element_type=jnp.float32
            )
            scores = scores * SCALE
            largest = new_largest_ref[:, lanes]
            acc, total = (new_acc_ref if last else acc_ref)[:, lanes], total_ref[:, lanes]
            if exact:
                before = largest
                largest = jnp.maximum(before, jnp.max(scores, axis=1, keepdims=True))
                rescale = jnp.exp2(before - largest)
                acc, total = acc * rescale, total * rescale
                new_largest_ref[:, lanes] = largest
            scores = scores - largest[:, :1]
            if not exact:
                highest = functools.reduce(
                    jnp.maximum,
                    [scores[start : start + BLK] for start in range(0, scores.shape[0], BLK)],
                )
                excess = highest if excess is None else jnp.maximum(excess, highest)
            weights = jnp.exp2(scores).astype(jnp.bfloat16)
            if last:
                weights_ref[head] = weights
                ones = jnp.ones((keys.shape[0], HEAD_DIM), weights.dtype)
                more = jnp.dot(weights, ones, preferred_element_type=jnp.float32)
                inverse_ref[:, lanes] = 1.0 / (total + more)
                if exact:
                    new_acc_ref[:, lanes] = acc
            else:
                values = jnp.concatenate([value_ref[:, lanes] for value_ref in value_refs], axis=0)
                more_acc, more = weigh(weights, values)
                new_acc_ref[:, lanes] = acc + more_acc
                new_total_ref[:, lanes] = total + more
        return excess

    excess = jnp.max(absorb(False))

    @pl.when(excess > LAZY)
    def _():
        absorb(True)


def value_kernel(scaled_ref, weights_ref, inverse_ref, *refs):
    value_refs, (out_hbm, out_ref, sems) = refs[:-3], refs[-3:]
    _, features = scaled_ref.shape
    copies = []
    for head in range(features // HEAD_DIM):
        lanes = slice(head * HEAD_DIM, (head + 1) * HEAD_DIM)
        values = jnp.concatenate([value_ref[:, lanes] for value_ref in value_refs], axis=0)
        attended = scaled_ref[:, lanes] + jnp.dot(
            weights_ref[head], values, preferred_element_type=jnp.float32
        )
        out_ref[:, lanes] = (attended * inverse_ref[:, lanes]).astype(out_ref.dtype)
        copies.append(
            pltpu.make_async_copy(out_ref.at[:, lanes], out_hbm.at[:, lanes], sems.at[head])
        )
        copies[-1].start()
    for copy in copies:
        copy.wait()


def hbm(array):
    return pltpu.with_memory_space_constraint(array, pltpu.HBM)


def swap(array, axis, distance):
    size = lax.axis_size(axis)
    return lax.ppermute(array, axis, [(i, i ^ distance) for i in range(size)])


def gather_pair(keys, values):
    return (keys, values), (swap(keys, "ctx", 1), swap(values, "ctx", 1))


def per_device(
    queries, own_keys, own_values, variant_blocks, db_keys, db_values, ret_shard, ret_block
):
    count, features = queries.shape[1:]
    heads = features // HEAD_DIM
    groups = lax.axis_size("dp")
    columns = lax.axis_size("ctx")
    slots = ret_shard.shape[1]
    tokens = slots * ROW_BLK
    capacity = max(2, 2 * slots // groups)
    me = lax.axis_index("dp").astype(jnp.int32).reshape(1)
    bf16 = jnp.bfloat16
    wide = jax.ShapeDtypeStruct((count, features), jnp.float32)
    piece = jax.ShapeDtypeStruct((2 * capacity * ROW_BLK, features), bf16)

    sent = pl.pallas_call(
        lambda *refs: pack_kernel(capacity, *refs),
        out_shape=[piece] * groups,
        in_specs=[SMEM] + [HBM] * 4,
        out_specs=[VMEM] * groups,
        scratch_shapes=[
            pltpu.VMEM(ret_shard.shape, jnp.int32),
            pltpu.VMEM(ret_block.shape, jnp.int32),
            pltpu.VMEM((2 * tokens, features), bf16),
            pltpu.SemaphoreType.DMA((4,)),
        ],
        name="pack",
        compiler_params=PARAMS,
    )(me, hbm(ret_shard), hbm(ret_block), hbm(db_keys[0]), hbm(db_values[0]))
    pieces = [sent[0]]
    for distance in range(1, groups):
        pieces.append(swap(sent[distance], "dp", distance))
    piece_rows = groups * piece.shape[0]
    query, acc, largest, total, choice = pl.pallas_call(
        lambda *refs: own_kernel(capacity, *refs),
        out_shape=[jax.ShapeDtypeStruct((count, features), bf16)]
        + [wide] * 3
        + [jax.ShapeDtypeStruct((2 * tokens, piece_rows), bf16)],
        in_specs=[SMEM] * 2 + [VMEM] + [HBM] * 3 + [VMEM],
        out_specs=[VMEM] * 5,
        scratch_shapes=[
            pltpu.VMEM((count, 2 * BLK), jnp.float32),
            pltpu.VMEM((count, features), bf16),
            pltpu.VMEM((count, features), bf16),
            pltpu.VMEM((count, features), bf16),
            pltpu.SemaphoreType.DMA((3,)),
        ],
        name="own",
        compiler_params=PARAMS,
        cost_estimate=pl.CostEstimate(
            flops=4 * count * 2 * BLK * features,
            transcendentals=2 * count * BLK * heads,
            bytes_accessed=20 * count * features,
        ),
    )(me, variant_blocks[0, 0], ret_shard, hbm(queries[0]), hbm(own_keys[0]), hbm(own_values[0]), sent[0])
    row_block = jax.ShapeDtypeStruct((tokens, features), bf16)
    keys, values = pl.pallas_call(
        compact_kernel,
        out_shape=[row_block] * 2,
        in_specs=[VMEM] * (1 + groups),
        out_specs=[VMEM] * 2,
        name="compact",
        compiler_params=PARAMS,
    )(choice, *pieces)
    far = []
    distance = columns // 2
    while distance > 1:
        far_keys = [swap(one, "ctx", distance) for one in [keys] + [k for k, _ in far]]
        far_values = [swap(one, "ctx", distance) for one in [values] + [v for _, v in far]]
        far = far + list(zip(far_keys, far_values))
        distance //= 2
    near = gather_pair(keys, values)
    far = [pair for one in far for pair in gather_pair(*one)]
    acc, largest, total = pl.pallas_call(
        lambda *refs: context_kernel(False, *refs),
        out_shape=[wide] * 3,
        in_specs=[VMEM] * (4 + 2 * len(near)),
        out_specs=[VMEM] * 3,
        input_output_aliases={2: 1},
        name="near",
        compiler_params=PARAMS,
    )(query, acc, largest, total, *[k for k, _ in near], *[v for _, v in near])
    weights, acc, largest, inverse = pl.pallas_call(
        lambda *refs: context_kernel(True, *refs),
        out_shape=[jax.ShapeDtypeStruct((heads, count, len(far) * tokens), bf16)] + [wide] * 3,
        in_specs=[VMEM] * (4 + len(far)),
        out_specs=[VMEM] * 4,
        input_output_aliases={1: 1, 2: 2},
        name="score",
        compiler_params=PARAMS,
    )(query, acc, largest, total, *[k for k, _ in far])
    attended = pl.pallas_call(
        value_kernel,
        out_shape=jax.ShapeDtypeStruct((count, features), bf16),
        in_specs=[VMEM] * (3 + len(far)),
        out_specs=HBM,
        scratch_shapes=[
            pltpu.VMEM((count, features), bf16),
            pltpu.SemaphoreType.DMA((heads,)),
        ],
        name="value",
        compiler_params=PARAMS,
    )(acc, weights, inverse, *[v for _, v in far])
    return attended[None]


def solution(mesh):
    split = P("dp", "ctx", None)
    return jax.shard_map(
        per_device,
        mesh=mesh,
        in_specs=(split,) * 6 + (P(None, "ctx"),) * 2,
        out_specs=split,
        check_vma=False,
    )
```

```python
import functools
import math

import jax
import jax.numpy as jnp
from jax import lax
from jax.experimental import pallas as pl
from jax.experimental.pallas import tpu as pltpu
from jax.sharding import PartitionSpec as P


HEAD_DIM = 128
BLK = 64
ROW_BLK = 4


PARAMS = pltpu.CompilerParams(vmem_limit_bytes=16 << 20)
SMEM = pl.BlockSpec(memory_space=pltpu.SMEM)
VMEM = pl.BlockSpec(memory_space=pltpu.VMEM)
HBM = pl.BlockSpec(memory_space=pltpu.HBM)
SCALE = math.log2(math.e) / math.sqrt(HEAD_DIM)
NT = (((1,), (1,)), ((), ()))
masked_score = -1e30


def iota(shape, dim):
    return lax.broadcasted_iota(jnp.int32, shape, dim)


def pick(matrix, rows):
    return jnp.dot(matrix.astype(jnp.bfloat16), rows, preferred_element_type=jnp.float32).astype(
        jnp.bfloat16
    )


def pack_kernel(capacity, me_ref, shard_hbm, block_hbm, keys_hbm, values_hbm, *refs):
    out_refs, (shard_ref, block_ref, rows_ref, sems) = refs[:-4], refs[-4:]
    me = me_ref[0]
    slots = shard_ref.shape[1]
    tokens = keys_hbm.shape[0]
    half = capacity * ROW_BLK
    copies = [
        pltpu.make_async_copy(source, target, sems.at[number])
        for number, (source, target) in enumerate(
            (
                (shard_hbm, shard_ref),
                (block_hbm, block_ref),
                (keys_hbm, rows_ref.at[0:tokens]),
                (values_hbm, rows_ref.at[tokens : 2 * tokens]),
            )
        )
    ]
    for copy in copies:
        copy.start()
    for copy in copies[:2]:
        copy.wait()
    row = iota((2 * half, slots), 0)
    level = (row % half) // ROW_BLK
    before = (iota((slots, slots), 0) < iota((slots, slots), 1)).astype(jnp.float32)
    mine_all = (shard_ref[...] == me).astype(jnp.float32)
    earlier_all = jnp.dot(mine_all, before, preferred_element_type=jnp.float32)
    wanted_all = jnp.where(mine_all > 0, earlier_all.astype(jnp.int32), -1)
    line = iota((2 * half, 1), 0)
    base = (line // half) * tokens + line % ROW_BLK
    column = iota((2 * half, 2 * tokens), 1)
    member = iota(wanted_all.shape, 0)
    choices = []
    for distance in range(len(out_refs) - 1):
        here = member == (me ^ distance)
        wanted = jnp.sum(jnp.where(here, wanted_all, 0), axis=0, keepdims=True)
        blocks = jnp.sum(jnp.where(here, block_ref[...], 0), axis=0, keepdims=True)
        source = jnp.sum(jnp.where(wanted == level, blocks, 0), axis=1, keepdims=True)
        choices.append((column == base + source * ROW_BLK).astype(jnp.bfloat16))
    choice = jnp.concatenate(choices, axis=0)
    for copy in copies[2:]:
        copy.wait()
    picked = pick(choice, rows_ref[...])
    for distance, out_ref in enumerate(out_refs[:-1]):
        first = distance * 2 * half
        out_ref[...] = picked[first : first + out_ref.shape[0]]
    first = last_distance(len(out_refs) - 1) * 2 * half + half
    out_refs[-1][...] = picked[first : first + half]


def context_choice(capacity, me, shards_all, columns):
    groups, slots = shards_all.shape
    half = capacity * ROW_BLK
    tokens = slots * ROW_BLK
    here = iota(shards_all.shape, 0) == me
    shards = jnp.sum(jnp.where(here, shards_all, 0), axis=0, keepdims=True)
    line = iota((2 * tokens, slots), 0)
    slot = (line % tokens) // ROW_BLK
    lane = iota((2 * tokens, slots), 1)
    named = jnp.sum(jnp.where(lane == slot, shards, 0), axis=1, keepdims=True)
    level = jnp.sum(((shards == named) & (lane < slot)).astype(jnp.int32), axis=1, keepdims=True)
    line = line[:, :1]
    distance = named ^ me
    last = last_distance(groups)
    place = jnp.where(distance > last, distance - 1, distance) * (2 * half)
    place = place + (line // tokens) * half
    place = jnp.where(distance == last, (groups - 1) * (2 * half), place)
    target = place + level * ROW_BLK + line % ROW_BLK
    return (iota((2 * tokens, columns), 1) == target).astype(jnp.bfloat16)


def last_distance(groups):
    return groups // 2


def compact_kernel(first, choice_ref, *refs):
    piece_refs, out_ref = refs[:-1], refs[-1]
    pieces = jnp.concatenate([piece_ref[...] for piece_ref in piece_refs], axis=0)
    out_ref[...] = pick(choice_ref[first : first + out_ref.shape[0], :], pieces)


def weigh(weights, values):
    both = jnp.concatenate([values, jnp.ones_like(values)], axis=1)
    result = jnp.dot(weights, both, preferred_element_type=jnp.float32)
    return result[:, :HEAD_DIM], result[:, HEAD_DIM:]


def own_heads(
    chosen,
    query_ref,
    keys_ref,
    values_ref,
    mask_ref,
    acc_ref,
    largest_ref,
    total_ref,
    weights_ref,
    ready,
):
    count = query_ref.shape[0]
    blocks = [slice(first, first + BLK) for first in range(0, count, BLK)]
    bands = [slice(max(0, rows.start - BLK), max(0, rows.start - BLK) + 2 * BLK) for rows in blocks]
    every = [slice(head * HEAD_DIM, (head + 1) * HEAD_DIM) for head in chosen]
    for lanes in every:
        for rows, band in zip(blocks, bands):
            acc_ref[rows, lanes] = lax.dot_general(
                query_ref[rows, lanes], keys_ref[band, lanes], NT, preferred_element_type=jnp.float32
            )
    for lanes in every:
        scores = acc_ref[:, lanes] * SCALE + mask_ref[...]
        largest = jnp.max(scores, axis=1, keepdims=True)
        weights_ref[:, lanes] = jnp.exp2(scores - largest).astype(jnp.bfloat16)
        largest_ref[:, lanes] = jnp.broadcast_to(largest, (count, HEAD_DIM))
    ready()
    for lanes in every:
        for rows, band in zip(blocks, bands):
            acc_ref[rows, lanes], total_ref[rows, lanes] = weigh(
                weights_ref[rows, lanes], values_ref[band, lanes]
            )


def own_first_kernel(
    capacity,
    chosen,
    me_ref,
    lengths_hbm,
    shard_hbm,
    q_hbm,
    keys_hbm,
    values_hbm,
    after_ref,
    query_ref,
    keys_ref,
    values_ref,
    mask_ref,
    choice_ref,
    acc_ref,
    largest_ref,
    total_ref,
    lengths_ref,
    shard_ref,
    weights_ref,
    sems,
):
    cut = len(chosen) * HEAD_DIM
    now, later = slice(0, cut), slice(cut, query_ref.shape[1])
    pairs = [(lengths_hbm, lengths_ref), (shard_hbm, shard_ref)]
    big = ((q_hbm, query_ref), (keys_hbm, keys_ref), (values_hbm, values_ref))
    for part in (now, later):
        pairs += [(source.at[:, part], target.at[:, part]) for source, target in big]
    copies = [
        pltpu.make_async_copy(source, target, sems.at[number])
        for number, (source, target) in enumerate(pairs)
    ]
    for copy in copies:
        copy.start()
    for copy in copies[:2]:
        copy.wait()
    choice_ref[...] = context_choice(capacity, me_ref[0], shard_ref[...], choice_ref.shape[1])
    row = iota((BLK, 2 * BLK), 0)
    column = iota((BLK, 2 * BLK), 1)
    mask_ref[0:BLK, :] = jnp.where(column <= row, 0.0, masked_score)
    for block in range(1, query_ref.shape[0] // BLK):
        end = jnp.int32(0)
        opens = jnp.int32(0)
        for variant in range(lengths_ref.shape[1]):
            end = end + lengths_ref[0, variant]
            opens = opens + (end == block).astype(jnp.int32)
        first = jnp.where(opens > 0, BLK, 0)
        allowed = (column <= row + BLK) & (column >= first)
        mask_ref[block * BLK : (block + 1) * BLK, :] = jnp.where(allowed, 0.0, masked_score)
    for copy in copies[2:4]:
        copy.wait()
    own_heads(
        chosen,
        query_ref,
        keys_ref,
        values_ref,
        mask_ref,
        acc_ref,
        largest_ref,
        total_ref,
        weights_ref,
        copies[4].wait,
    )
    for copy in copies[5:]:
        copy.wait()


def own_rest_kernel(chosen, query_ref, keys_ref, values_ref, mask_ref, after_ref, *refs):
    own_heads(chosen, query_ref, keys_ref, values_ref, mask_ref, *refs[3:], lambda: None)


LAZY = 60.0


def context_kernel(last, query_ref, acc_ref, largest_ref, total_ref, *refs):
    out_count = 4 if last else 3
    refs, out_refs = refs[:-out_count], refs[-out_count:]
    if last:
        key_refs, value_refs = refs, None
        weights_ref, new_acc_ref, new_largest_ref, inverse_ref = out_refs
    else:
        key_refs, value_refs = refs[: len(refs) // 2], refs[len(refs) // 2 :]
        new_acc_ref, new_largest_ref, new_total_ref = out_refs
    features = query_ref.shape[1]

    def absorb(exact):
        excess = None
        for head in range(features // HEAD_DIM):
            lanes = slice(head * HEAD_DIM, (head + 1) * HEAD_DIM)
            keys = jnp.concatenate([key_ref[:, lanes] for key_ref in key_refs], axis=0)
            scores = lax.dot_general(
                query_ref[:, lanes], keys, NT, preferred_element_type=jnp.float32
            )
            scores = scores * SCALE
            largest = new_largest_ref[:, lanes]
            acc, total = (new_acc_ref if last else acc_ref)[:, lanes], total_ref[:, lanes]
            if exact:
                before = largest
                largest = jnp.maximum(before, jnp.max(scores, axis=1, keepdims=True))
                rescale = jnp.exp2(before - largest)
                acc, total = acc * rescale, total * rescale
                new_largest_ref[:, lanes] = largest
            scores = scores - largest[:, :1]
            if not exact:
                highest = functools.reduce(
                    jnp.maximum,
                    [scores[start : start + BLK] for start in range(0, scores.shape[0], BLK)],
                )
                excess = highest if excess is None else jnp.maximum(excess, highest)
            weights = jnp.exp2(scores).astype(jnp.bfloat16)
            if last:
                weights_ref[head] = weights
                ones = jnp.ones((keys.shape[0], HEAD_DIM), weights.dtype)
                more = jnp.dot(weights, ones, preferred_element_type=jnp.float32)
                inverse_ref[:, lanes] = 1.0 / (total + more)
                if exact:
                    new_acc_ref[:, lanes] = acc
            else:
                values = jnp.concatenate([value_ref[:, lanes] for value_ref in value_refs], axis=0)
                more_acc, more = weigh(weights, values)
                new_acc_ref[:, lanes] = acc + more_acc
                new_total_ref[:, lanes] = total + more
        return excess

    excess = jnp.max(absorb(False))

    @pl.when(excess > LAZY)
    def _():
        absorb(True)


def value_kernel(scaled_ref, weights_ref, inverse_ref, *refs):
    value_refs, (out_hbm, out_ref, sems) = refs[:-3], refs[-3:]
    _, features = scaled_ref.shape
    copies = []
    for head in range(features // HEAD_DIM):
        lanes = slice(head * HEAD_DIM, (head + 1) * HEAD_DIM)
        values = jnp.concatenate([value_ref[:, lanes] for value_ref in value_refs], axis=0)
        attended = scaled_ref[:, lanes] + jnp.dot(
            weights_ref[head], values, preferred_element_type=jnp.float32
        )
        out_ref[:, lanes] = (attended * inverse_ref[:, lanes]).astype(out_ref.dtype)
        copies.append(
            pltpu.make_async_copy(out_ref.at[:, lanes], out_hbm.at[:, lanes], sems.at[head])
        )
        copies[-1].start()
    for copy in copies:
        copy.wait()


def hbm(array):
    return pltpu.with_memory_space_constraint(array, pltpu.HBM)


def swap(array, axis, distance):
    size = lax.axis_size(axis)
    return lax.ppermute(array, axis, [(i, i ^ distance) for i in range(size)])


def gather_pair(keys, values):
    return (keys, values), (swap(keys, "ctx", 1), swap(values, "ctx", 1))


def per_device(
    queries, own_keys, own_values, variant_blocks, db_keys, db_values, ret_shard, ret_block
):
    count, features = queries.shape[1:]
    heads = features // HEAD_DIM
    groups = lax.axis_size("dp")
    columns = lax.axis_size("ctx")
    slots = ret_shard.shape[1]
    tokens = slots * ROW_BLK
    capacity = max(2, 2 * slots // groups)
    me = lax.axis_index("dp").astype(jnp.int32).reshape(1)
    bf16 = jnp.bfloat16
    wide = jax.ShapeDtypeStruct((count, features), jnp.float32)
    piece = jax.ShapeDtypeStruct((2 * capacity * ROW_BLK, features), bf16)

    last = last_distance(groups)
    part = jax.ShapeDtypeStruct((capacity * ROW_BLK, features), bf16)
    sent = pl.pallas_call(
        lambda *refs: pack_kernel(capacity, *refs),
        out_shape=[piece] * last + [part] + [piece] * (groups - 1 - last) + [part],
        in_specs=[SMEM] + [HBM] * 4,
        out_specs=[VMEM] * (groups + 1),
        scratch_shapes=[
            pltpu.VMEM(ret_shard.shape, jnp.int32),
            pltpu.VMEM(ret_block.shape, jnp.int32),
            pltpu.VMEM((2 * tokens, features), bf16),
            pltpu.SemaphoreType.DMA((4,)),
        ],
        name="pack",
        compiler_params=PARAMS,
    )(me, hbm(ret_shard), hbm(ret_block), hbm(db_keys[0]), hbm(db_values[0]))
    pieces = [sent[0]]
    for distance in range(1, groups):
        pieces.append(swap(sent[distance], "dp", distance))
    last_values = swap(sent[groups], "dp", last)
    last_keys = pieces.pop(last)

    stack_rows = (groups - 1) * piece.shape[0] + part.shape[0]
    row_block = jax.ShapeDtypeStruct((tokens, features), bf16)

    def compact(first, choice, *stack):
        return pl.pallas_call(
            lambda *refs: compact_kernel(first, *refs),
            out_shape=row_block,
            in_specs=[VMEM] * (1 + len(stack)),
            out_specs=VMEM,
            compiler_params=PARAMS,
        )(choice, *stack)

    soon = range(heads // 2)
    rows_like = jax.ShapeDtypeStruct((count, features), bf16)
    query, own_k, own_v, mask, choice, *state = pl.pallas_call(
        lambda *refs: own_first_kernel(capacity, soon, *refs),
        out_shape=[rows_like] * 3
        + [
            jax.ShapeDtypeStruct((count, 2 * BLK), jnp.float32),
            jax.ShapeDtypeStruct((2 * tokens, stack_rows), bf16),
        ]
        + [wide] * 3,
        in_specs=[SMEM] + [HBM] * 5 + [VMEM],
        out_specs=[VMEM] * 8,
        scratch_shapes=[
            pltpu.SMEM(variant_blocks.shape[1:], jnp.int32),
            pltpu.VMEM(ret_shard.shape, jnp.int32),
            pltpu.VMEM((count, features), bf16),
            pltpu.SemaphoreType.DMA((8,)),
        ],
        name="own_first",
        compiler_params=PARAMS,
        cost_estimate=pl.CostEstimate(
            flops=4 * count * BLK * features,
            transcendentals=count * BLK * heads,
            bytes_accessed=10 * count * features,
        ),
    )(
        me,
        hbm(variant_blocks[0]),
        hbm(ret_shard),
        hbm(queries[0]),
        hbm(own_keys[0]),
        hbm(own_values[0]),
        sent[0],
    )
    keys = compact(0, choice, *pieces, last_keys)
    values = compact(tokens, choice, *pieces, last_values)
    acc, largest, total = pl.pallas_call(
        lambda *refs: own_rest_kernel(range(len(soon), heads), *refs),
        out_shape=[wide] * 3,
        in_specs=[VMEM] * 8,
        out_specs=[VMEM] * 3,
        scratch_shapes=[pltpu.VMEM((count, features), bf16)],
        input_output_aliases={5: 0, 6: 1, 7: 2},
        name="own_rest",
        compiler_params=PARAMS,
    )(query, own_k, own_v, mask, values, *state)
    far = []
    distance = columns // 2
    while distance > 1:
        far_keys = [swap(one, "ctx", distance) for one in [keys] + [k for k, _ in far]]
        far_values = [swap(one, "ctx", distance) for one in [values] + [v for _, v in far]]
        far = far + list(zip(far_keys, far_values))
        distance //= 2
    near = gather_pair(keys, values)
    far = [pair for one in far for pair in gather_pair(*one)]
    acc, largest, total = pl.pallas_call(
        lambda *refs: context_kernel(False, *refs),
        out_shape=[wide] * 3,
        in_specs=[VMEM] * (4 + 2 * len(near)),
        out_specs=[VMEM] * 3,
        input_output_aliases={2: 1},
        name="near",
        compiler_params=PARAMS,
    )(query, acc, largest, total, *[k for k, _ in near], *[v for _, v in near])
    weights, acc, largest, inverse = pl.pallas_call(
        lambda *refs: context_kernel(True, *refs),
        out_shape=[jax.ShapeDtypeStruct((heads, count, len(far) * tokens), bf16)] + [wide] * 3,
        in_specs=[VMEM] * (4 + len(far)),
        out_specs=[VMEM] * 4,
        input_output_aliases={1: 1, 2: 2},
        name="score",
        compiler_params=PARAMS,
    )(query, acc, largest, total, *[k for k, _ in far])
    attended = pl.pallas_call(
        value_kernel,
        out_shape=jax.ShapeDtypeStruct((count, features), bf16),
        in_specs=[VMEM] * (3 + len(far)),
        out_specs=HBM,
        scratch_shapes=[
            pltpu.VMEM((count, features), bf16),
            pltpu.SemaphoreType.DMA((heads,)),
        ],
        name="value",
        compiler_params=PARAMS,
    )(acc, weights, inverse, *[v for _, v in far])
    return attended[None]


def solution(mesh):
    split = P("dp", "ctx", None)
    return jax.shard_map(
        per_device,
        mesh=mesh,
        in_specs=(split,) * 6 + (P(None, "ctx"),) * 2,
        out_specs=split,
        check_vma=False,
    )
```
